32 devices in a mesh: space: 16 (over z, y, core), modes: 2 (over x).
Axes of the slice: x: 2, y: 2, z: 4, core: 2. Of those that a mesh axis runs over, the one named last changes fastest.
Arguments:
- initial_heat_weights: float32 [120, 16, 32, 128], P('modes', 'space'), may hold values from -6 to 6
- source_weights: float32 [120, 16, 32, 128], P('modes', 'space'), may hold values from -12 to 12
- heat_storage_slope: float32 [16, 32, 128], P('space'), may hold values from 1 to 8
- average_diffusivity: float32 [16, 32, 128], P('space'), may hold values from 0.5 to 2
- metal_indicator: int32 [16, 32, 128], P('space'), may hold values 0 or 1
- uncertain_diffusivity_fields: float32 [7, 16, 32, 128], P(None, 'space'), may hold values from -0.6 to 0.6
- basis_index_pairs: int32 [7, 72, 2], replicated, may hold values from 0 to 119
- basis_integral_entries: float32 [7, 72], replicated, may hold values from -3 to 3
Outputs:
- refined_heat_weights: float32 [120, 16, 32, 128], P('modes', 'space')
- residual: float32 [120, 16, 32, 128], P('modes', 'space')
The draws below stay inside these ranges and needn't reach their ends.
Inputs may be any that keep to these rules, and one draw needn't show every extreme that they name: `basis_index_pairs`: pairs may repeat.
All inputs are finite; a program needn't handle non-finite values. No bound on the sum of `metal_indicator` on one device may be relied on, other than what follows from the above.
Results may differ from the reference program's by a relative error of at most 0.00024.
Values sent between devices are 32-bit elements; how exact they have to be, the bound alone decides.
No kernel may reach another device: no remote copies, remote signals or barrier semaphores. Data moves between devices by JAX's collectives and lax.ppermute only.
A program may use at most 64 MiB of HBM per device.

```python
import math
import jax
import jax.numpy as jnp
from jax import lax

BASIS_SIZE = 120
KL = 7
PAIRS = 72
GRID_LENGTH_Y = 32
GRID_LENGTH_Z = 128
ROUNDS = 2
GRID_LENGTH_X = 16


def place_ends(result, key, smallest, top_value):
    longest = result.shape.index(max(result.shape))
    spots = []
    for shift in (0, 1):
        where = [jax.random.randint(jax.random.fold_in(key, axis), (), 0, length) for axis, length in enumerate(result.shape)]
        where[longest] = (where[longest] + shift) % result.shape[longest]
        spots.append(tuple(where))
    return result.at[spots[0]].set(smallest).at[spots[1]].set(top_value)


def steps_of(rng, extent, split, least, largest):
    level = 1.0
    for axis_at, shards_of in split:
        heights = jax.random.uniform(jax.random.fold_in(jax.random.fold_in(rng, 6), axis_at), (shards_of,), jnp.float32, least / len(split), largest / len(split))
        level = level * jnp.repeat(jnp.exp(heights), extent[axis_at] // shards_of).reshape((-1,) + (1,) * (len(extent) - 1 - axis_at))
    return level


def noise(own_key, shape, scale, limit, pieces=(), kind=jnp.bfloat16):
    gain = steps_of(own_key, shape, pieces, -0.22, 0.18) if pieces else 1.0
    drawn = jax.random.normal(own_key, shape, jnp.float32) * scale * gain
    return jnp.minimum(jnp.maximum(drawn, -limit), limit).astype(kind)


def setup_inputs(seed: int = 0) -> dict:
    arg_keys = jax.random.split(jax.random.key(seed), 9)
    initial_heat_weights = noise(arg_keys[0], (BASIS_SIZE, GRID_LENGTH_X, GRID_LENGTH_Y, GRID_LENGTH_Z), 1.0, 6.0, ((0, 2), (1, 16)), jnp.float32)
    source_weights = noise(arg_keys[1], (BASIS_SIZE, GRID_LENGTH_X, GRID_LENGTH_Y, GRID_LENGTH_Z), 2.0, 12.0, ((0, 2), (1, 16)), jnp.float32)
    heat_storage_slope = jnp.clip(jnp.exp(math.log(8.0) - 2.0794415 * jax.random.uniform(arg_keys[2], (GRID_LENGTH_X, GRID_LENGTH_Y, GRID_LENGTH_Z), jnp.float32) ** steps_of(arg_keys[2], (GRID_LENGTH_X, GRID_LENGTH_Y, GRID_LENGTH_Z), ((0, 16),), -0.2, 0.2)), 1.0, 8.0)
    average_diffusivity = jnp.clip(jnp.exp(math.log(2.0) - 1.3862944 * jax.random.uniform(arg_keys[3], (GRID_LENGTH_X, GRID_LENGTH_Y, GRID_LENGTH_Z), jnp.float32) ** steps_of(arg_keys[3], (GRID_LENGTH_X, GRID_LENGTH_Y, GRID_LENGTH_Z), ((0, 16),), -0.2, 0.2)), 0.5, 2.0)
    metal_indicator = place_ends((jax.random.randint(arg_keys[4], (GRID_LENGTH_X, GRID_LENGTH_Y, GRID_LENGTH_Z), 0, 4) < 1).astype(jnp.int32), jax.random.fold_in(arg_keys[4], 1), 0, 1)
    uncertain_diffusivity_fields = noise(arg_keys[5], (KL, GRID_LENGTH_X, GRID_LENGTH_Y, GRID_LENGTH_Z), 0.2, 0.6, ((1, 16),), jnp.float32)
    basis_index_pairs = place_ends(jax.random.randint(arg_keys[6], (KL, PAIRS, 2), 0, BASIS_SIZE), jax.random.fold_in(arg_keys[6], 1), 0, BASIS_SIZE - 1).astype(jnp.int32)
    basis_integral_entries = noise(arg_keys[7], (KL, PAIRS), 0.5, 3.0, (), jnp.float32)
    return {"initial_heat_weights": initial_heat_weights, "source_weights": source_weights, "heat_storage_slope": heat_storage_slope, "average_diffusivity": average_diffusivity, "metal_indicator": metal_indicator, "uncertain_diffusivity_fields": uncertain_diffusivity_fields, "basis_index_pairs": basis_index_pairs, "basis_integral_entries": basis_integral_entries}


relaxation = 0.8


def neighbour_form(field):
    beside_all = jnp.roll(field, 1, -3) + jnp.roll(field, -1, -3)
    beside_all = beside_all + jnp.roll(field, 1, -2) + jnp.roll(field, -1, -2)
    beside_all = beside_all + jnp.roll(field, 1, -1) + jnp.roll(field, -1, -1)
    return 6.0 * field - beside_all


def coupling_matrices(basis_index_pairs, basis_integral_entries):
    indices = jnp.arange(BASIS_SIZE, dtype=jnp.int32)
    row_hits = (basis_index_pairs[:, :, 0][:, :, None] == indices).astype(jnp.float32)
    col_hits = (basis_index_pairs[:, :, 1][:, :, None] == indices).astype(jnp.float32)
    return jnp.einsum("kpi,kp,kpj->kij", row_hits, basis_integral_entries, col_hits, precision=lax.Precision.HIGHEST)


def apply_operator(field, heat_storage_slope, mean_cond, uncertain_diffusivity_fields, matrices):
    total = heat_storage_slope * field + mean_cond * neighbour_form(field)

    def add_term(running, inputs):
        matrix, coeff = inputs
        mixed = jnp.einsum("ij,jxyz->ixyz", matrix, field, precision=lax.Precision.HIGHEST)
        return running + coeff * neighbour_form(mixed), None

    total, unused = lax.scan(add_term, total, (matrices, uncertain_diffusivity_fields))
    return total


def reference(initial_heat_weights, source_weights, heat_storage_slope, average_diffusivity, metal_indicator, uncertain_diffusivity_fields, basis_index_pairs, basis_integral_entries):
    matrices = coupling_matrices(basis_index_pairs, basis_integral_entries)
    mean_cond = average_diffusivity * (1.0 + 3.0 * metal_indicator.astype(average_diffusivity.dtype))
    scaling = 1.0 / (heat_storage_slope + 6.0 * mean_cond)
    refined_heat_weights = initial_heat_weights
    residual = source_weights
    for turn in range(ROUNDS):
        residual = source_weights - apply_operator(refined_heat_weights, heat_storage_slope, mean_cond, uncertain_diffusivity_fields, matrices)
        refined_heat_weights = refined_heat_weights + relaxation * scaling * residual
    return refined_heat_weights, residual
```

```python
import functools

import jax
import jax.numpy as jnp
from jax import lax
from jax.experimental import pallas as pl
from jax.experimental.pallas import tpu as pltpu
from jax.sharding import PartitionSpec as P

BASIS_SIZE = 120
ROUNDS = 2
RELAXATION = 0.8
ROWS = 8
F32, BF16 = jnp.float32, jnp.bfloat16


def ceil_to(value, unit):
    return -(-value // unit) * unit


def group_of(n):
    return max(g for g in range(1, 7) if n % g == 0)


def params():
    return pltpu.CompilerParams(vmem_limit_bytes=12 * 1024 * 1024)


def vmem():
    return pl.BlockSpec(memory_space=pltpu.VMEM)


def lap_kernel(n, prev, cur, nxt, near, far, out):
    nz = cur.shape[1]
    g = group_of(n)
    row = lax.broadcasted_iota(jnp.int32, (g, ROWS, nz), 1)
    for j in range(0, n, g):
        rows = pl.ds(j * ROWS, g * ROWS)
        take = lambda ref: ref[rows, :].reshape(g, ROWS, nz)
        x = take(cur)
        up = jnp.where(row == 0, pltpu.roll(take(prev), 1, 1), pltpu.roll(x, 1, 1))
        down = jnp.where(
            row == ROWS - 1,
            pltpu.roll(take(nxt), ROWS - 1, 1),
            pltpu.roll(x, ROWS - 1, 1),
        )
        sides = pltpu.roll(x, 1, 2) + pltpu.roll(x, nz - 1, 2)
        beside = (up + down) + sides + (take(near) + take(far))
        out[rows, :] = (6.0 * x - beside).reshape(g * ROWS, nz)


def couple(n, chunk, fields, matrix, lap, rhs, mixed, emit):
    nz = lap.shape[1]
    kl = fields.shape[0]
    wide, tall = ceil_to(n, 16), ceil_to(n, 8)
    for pair in range(ROWS // 2):
        slot = pair % 2
        for half in range(2):
            y = 2 * pair + half
            v = lap[pl.ds(y, n, stride=ROWS), :]
            hi = v.astype(BF16)
            lo = (v - hi.astype(F32)).astype(BF16)
            cols = pl.ds(half * nz, nz)
            rhs[slot, pl.ds(0, n), cols] = hi
            rhs[slot, pl.ds(wide, n), cols] = lo
            rhs[slot, pl.ds(2 * wide, n), cols] = hi
        mixed[slot] = jnp.dot(
            matrix[...], rhs[slot], preferred_element_type=F32
        )
        for half in range(2):
            y = 2 * pair + half
            cols = pl.ds(half * nz, nz)
            total = None
            for k in range(kl):
                field = fields[k, pl.ds(chunk * ROWS + y, 1), :]
                term = field * mixed[slot, pl.ds(k * tall, n), cols]
                total = term if total is None else total + term
            emit(y, total)


def clear_rhs(n, rhs):
    wide = ceil_to(n, 16)
    if wide != n:
        rhs[...] = jnp.zeros_like(rhs)


def own_kernel(n, chunk, fields, matrix, lap, out, rhs, mixed):
    clear_rhs(n, rhs)

    def emit(y, total):
        out[pl.ds(y, n, stride=ROWS), :] = total

    couple(n, chunk, fields, matrix, lap, rhs, mixed, emit)


def final_kernel(n, chunk, others, last, *refs):
    fields, slope, average, metal, matrices, source, field, lap, own = refs[:9]
    laps = refs[9 : 9 + others]
    outs = refs[9 + others : -3]
    outs = outs[2:] if last and len(outs) == 4 else outs
    rhs, mixed, total_ref = refs[-3:]
    nz = lap.shape[1]
    clear_rhs(n, rhs)
    for index in range(others):
        base = own if index == 0 else total_ref

        def emit(y, total):
            at = pl.ds(y, n, stride=ROWS)
            total_ref[at, :] = base[at, :] + total

        couple(n, chunk, fields, matrices.at[index], laps[index], rhs, mixed, emit)
    at = pl.ds(chunk * ROWS, ROWS)
    slope_here = slope[at, :]
    cond = average[at, :] * (1.0 + 3.0 * metal[at, :].astype(F32))
    step = RELAXATION * (1.0 / (slope_here + 6.0 * cond))
    g = group_of(n)
    for j in range(0, n, g):
        rows = pl.ds(j * ROWS, g * ROWS)
        take = lambda ref: ref[rows, :].reshape(g, ROWS, nz)
        u = take(field)
        rest = slope_here * u + (cond * take(lap) + take(total_ref))
        residual = source[pl.ds(j, g)] - rest
        u = u + step * residual
        if last:
            outs[0][pl.ds(j, g)] = u
            outs[1][pl.ds(j, g)] = residual
        else:
            outs[0][rows, :] = u.reshape(g * ROWS, nz)


def scratch(n, kl, nz):
    wide, tall = ceil_to(n, 16), ceil_to(n, 8)
    return [
        pltpu.VMEM((2, 3 * wide, 2 * nz), BF16),
        pltpu.VMEM((2, kl * tall, 2 * nz), F32),
    ]


def lap_call(n, prev, cur, nxt, near, far):
    return pl.pallas_call(
        functools.partial(lap_kernel, n),
        out_shape=jax.ShapeDtypeStruct(cur.shape, F32),
        in_specs=[vmem()] * 5,
        out_specs=vmem(),
        compiler_params=params(),
        name="lap",
        cost_estimate=pl.CostEstimate(
            flops=12 * cur.size, bytes_accessed=24 * cur.size, transcendentals=0
        ),
    )(prev, cur, nxt, near, far)


def own_call(n, chunk, fields, matrix, lap):
    kl = fields.shape[0]
    return pl.pallas_call(
        functools.partial(own_kernel, n, chunk),
        out_shape=jax.ShapeDtypeStruct(lap.shape, F32),
        in_specs=[vmem()] * 3,
        out_specs=vmem(),
        scratch_shapes=scratch(n, kl, lap.shape[1]),
        compiler_params=params(),
        name="own",
        cost_estimate=pl.CostEstimate(
            flops=2 * matrix.size * lap.size // n,
            bytes_accessed=8 * lap.size,
            transcendentals=0,
        ),
    )(fields, matrix, lap)


def final_call(n, chunk, last, shared, matrices, source, field, lap, own, laps, outs):
    fields, slope, average, metal = shared
    nz = lap.shape[1]
    block = pl.BlockSpec((n, ROWS, nz), lambda i: (0, chunk, 0))
    whole = lambda a: pl.BlockSpec(a.shape, lambda i, d=a.ndim: (0,) * d)
    operands = [fields, slope, average, metal, matrices, source, field, lap, own, *laps]
    specs = [block if a is source else whole(a) for a in operands]
    aliases = {}
    if last:
        shapes = [jax.ShapeDtypeStruct(source.shape, F32)] * 2
        out_specs = [block] * 2
        if outs:
            aliases = {len(operands) + i: i for i in range(2)}
            operands += list(outs)
            specs += [pl.BlockSpec(memory_space=pl.ANY)] * 2
    else:
        shapes = [jax.ShapeDtypeStruct(lap.shape, F32)]
        out_specs = [whole(lap)]
    return pl.pallas_call(
        functools.partial(final_kernel, n, chunk, len(laps), last),
        grid=(1,),
        out_shape=shapes,
        in_specs=specs,
        out_specs=out_specs,
        scratch_shapes=scratch(n, fields.shape[0], nz) + [pltpu.VMEM(lap.shape, F32)],
        input_output_aliases=aliases,
        compiler_params=params(),
        name="final",
        cost_estimate=pl.CostEstimate(
            flops=2 * matrices.size * lap.size // n,
            bytes_accessed=24 * lap.size,
            transcendentals=0,
        ),
    )(*operands)


def near_swap(x):
    count = lax.axis_size("space")
    return lax.ppermute(x, "space", [(i, i ^ 1) for i in range(count)])


def far_swap(x):
    count = lax.axis_size("space")
    pairs = [(i, (i + (1 if i % 2 else -1)) % count) for i in range(count)]
    return lax.ppermute(x, "space", pairs)


def to_others(x):
    count = lax.axis_size("modes")
    return [
        lax.ppermute(x, "modes", [(i, (i + s) % count) for i in range(count)])
        for s in range(1, count)
    ]


def coupling(pairs, entries, n):
    count = lax.axis_size("modes")
    me = lax.axis_index("modes")
    wide, tall = ceil_to(n, 16), ceil_to(n, 8)
    kl = pairs.shape[0]
    inside = jnp.arange(tall) < n
    own_rows = jnp.where(inside, me * n + jnp.arange(tall), -1)
    shifts = jnp.arange(count)
    starts = jnp.remainder(me - shifts, count) * n
    lanes = jnp.arange(wide)
    columns = jnp.where(lanes < n, starts[:, None] + lanes, -1).reshape(-1)
    row_hits = (pairs[:, :, 0][:, :, None] == own_rows).astype(F32)
    col_hits = (pairs[:, :, 1][:, :, None] == columns).astype(F32)
    g = jnp.einsum(
        "kpi,kp,kpj->kij", row_hits, entries, col_hits, precision=lax.Precision.HIGHEST
    )
    hi = lax.reduce_precision(g, 8, 7)
    lo = g - hi
    parts = [
        part.astype(BF16).reshape(kl * tall, count, wide).transpose(1, 0, 2)
        for part in (hi, hi, lo)
    ]
    return jnp.concatenate(parts, axis=-1)


def on_device(
    initial_heat_weights,
    source_weights,
    heat_storage_slope,
    average_diffusivity,
    metal_indicator,
    uncertain_diffusivity_fields,
    basis_index_pairs,
    basis_integral_entries,
):
    n, planes, ny, nz = initial_heat_weights.shape
    assert planes == 1 and ny % ROWS == 0
    count = ny // ROWS
    u0 = initial_heat_weights[:, 0]
    source = source_weights[:, 0]
    shared = (
        uncertain_diffusivity_fields[:, 0],
        heat_storage_slope[0],
        average_diffusivity[0],
        metal_indicator[0],
    )
    field = [
        u0[:, c * ROWS : (c + 1) * ROWS].reshape(n * ROWS, nz) for c in range(count)
    ]
    matrices = coupling(basis_index_pairs, basis_integral_entries, n)
    outs = ()
    for turn in range(ROUNDS):
        last = turn == ROUNDS - 1
        order = [(c + turn) % count for c in range(count)]
        halos = {c: (near_swap(field[c]), far_swap(field[c])) for c in order}
        new = [None] * count
        for c in order:
            lap = lap_call(
                n, field[c - 1], field[c], field[(c + 1) % count], *halos[c]
            )
            laps = to_others(lap)
            own = own_call(n, c, shared[0], matrices[0], lap)
            got = final_call(
                n, c, last, shared, matrices[1:], source, field[c], lap, own, laps, outs
            )
            if last:
                outs = got
            else:
                new[c] = got[0]
        field = new
    return (outs[0][:, None], outs[1][:, None])


def solution(mesh):
    placed = (
        P("modes", "space", None, None),
        P("modes", "space", None, None),
        P("space", None, None),
        P("space", None, None),
        P("space", None, None),
        P(None, "space", None, None),
        P(),
        P(),
    )
    return jax.shard_map(
        on_device,
        mesh=mesh,
        in_specs=placed,
        out_specs=(P("modes", "space", None, None), P("modes", "space", None, None)),
        check_vma=False,
    )
```

```python
import functools

import jax
import jax.numpy as jnp
from jax import lax
from jax.experimental import pallas as pl
from jax.experimental.pallas import tpu as pltpu
from jax.sharding import PartitionSpec as P


ROUNDS = 2
RELAXATION = 0.8
ROWS = 8
F32, BF16 = jnp.float32, jnp.bfloat16


def ceil_to(value, unit):
    return -(-value // unit) * unit


def group_of(n):
    return max(g for g in range(1, 7) if n % g == 0)


def params():
    return pltpu.CompilerParams(vmem_limit_bytes=6 * 1024 * 1024)


def vmem():
    return pl.BlockSpec(memory_space=pltpu.VMEM)


def cell_factors(chunk, slope, average, metal):
    at = pl.ds(chunk * ROWS, ROWS)
    here = slope[at, :]
    cond = average[at, :] * (1.0 + 3.0 * metal[at, :].astype(F32))
    return here, cond, RELAXATION * (1.0 / (here + 6.0 * cond))


def lap_kernel(n, chunk, slots, edge, compact, prev, cur, nxt, near, far, out):
    nz = cur.shape[1]
    g = group_of(n)
    row = lax.broadcasted_iota(jnp.int32, (g, ROWS, nz), 1)
    for j in range(0, n, g):

        def take(ref, slot):
            return ref[pl.ds((slot * n + j) * ROWS, g * ROWS), :].reshape(g, ROWS, nz)

        def handed(ref):
            rows = [ref[pl.ds(n * ROWS + j + i, 1), :] for i in range(g)]
            return jnp.stack([jnp.broadcast_to(r, (ROWS, nz)) for r in rows])

        x = take(cur, slots[1])
        if compact:
            before, after = handed(prev), handed(nxt)
        else:
            before = pltpu.roll(take(prev, slots[0]), 1, 1)
            after = pltpu.roll(take(nxt, slots[2]), ROWS - 1, 1)
        if len(near.shape) == 3:
            inside = near[pl.ds(j, g), pl.ds(chunk * ROWS, ROWS), :]
        else:
            inside = take(near, slots[3])
        up = jnp.where(row == 0, before, pltpu.roll(x, 1, 1))
        down = jnp.where(row == ROWS - 1, after, pltpu.roll(x, ROWS - 1, 1))
        sides = pltpu.roll(x, 1, 2) + pltpu.roll(x, nz - 1, 2)
        beside = (up + down) + sides + (inside + take(far, slots[4]))
        out[pl.ds(j * ROWS, g * ROWS), :] = (6.0 * x - beside).reshape(g * ROWS, nz)
    if edge is not None:
        start = slots[1] * n * ROWS + edge
        out[pl.ds(n * ROWS, n), :] = cur[pl.ds(start, n, stride=ROWS), :]


def couple(n, chunk, blocks, fields, matrix, lap, rhs, mixed, emit):
    nz = lap.shape[1]
    kl = fields.shape[0]
    wide, tall = ceil_to(n, 16), ceil_to(n, 8)
    used = pl.ds(0, blocks * kl * tall)
    for pair in range(ROWS // 2):
        slot = pair % 2
        for half in range(2):
            v = lap[pl.ds(2 * pair + half, n, stride=ROWS), :]
            hi = v.astype(BF16)
            lo = (v - hi.astype(F32)).astype(BF16)
            cols = pl.ds(half * nz, nz)
            rhs[slot, pl.ds(0, n), cols] = hi
            rhs[slot, pl.ds(wide, n), cols] = lo
            rhs[slot, pl.ds(2 * wide, n), cols] = hi
        mixed[slot] = jnp.dot(matrix[used, :], rhs[slot], preferred_element_type=F32)
        for half in range(2):
            y = 2 * pair + half
            cols = pl.ds(half * nz, nz)
            for b in range(blocks):
                total = None
                for k in range(kl):
                    field = fields[k, pl.ds(chunk * ROWS + y, 1), :]
                    at = pl.ds((b * kl + k) * tall, n)
                    term = field * mixed[slot, at, cols]
                    total = term if total is None else total + term
                emit(y, b, total)


def clear_rhs(n, rhs):
    if ceil_to(n, 16) != n:
        rhs[...] = jnp.zeros_like(rhs)


def own_kernel(n, chunk, blocks, fields, matrices, lap, out, rhs, mixed):
    clear_rhs(n, rhs)

    def emit(y, b, total):
        out[pl.ds(b * n * ROWS + y, n, stride=ROWS), :] = total

    couple(n, chunk, blocks, fields, matrices.at[0], lap, rhs, mixed, emit)


def blend_kernel(n, chunk, slope, average, metal, field, source, out):
    nz = field.shape[1]
    here, _, step = cell_factors(chunk, slope, average, metal)
    g = group_of(n)
    for j in range(0, n, g):
        rows = pl.ds(j * ROWS, g * ROWS)
        u = field[rows, :].reshape(g, ROWS, nz)
        v = u + step * (source[pl.ds(j, g)] - here * u)
        out[rows, :] = v.reshape(g * ROWS, nz)


def final_kernel(n, chunk, slot, others, last, double, *refs):
    fields, slope, average, metal, matrices, source, field, lap, own = refs[:9]
    laps, refs = refs[9 : 9 + others], refs[9 + others :]
    blended, refs = (refs[0], refs[1:]) if double else (None, refs)
    outs, (rhs, mixed, sums) = refs[:-3], refs[-3:]
    outs = outs[2:] if len(outs) == 4 else outs
    nz = lap.shape[1]
    clear_rhs(n, rhs)
    for other in range(others):
        base = own if other == 0 else sums

        def emit(y, b, total):
            at = pl.ds(b * n * ROWS + y, n, stride=ROWS)
            sums[at, :] = base[at, :] + total

        blocks = 2 if double else 1
        couple(
            n, chunk, blocks, fields, matrices.at[1 + other], laps[other], rhs, mixed, emit
        )
    here, cond, step = cell_factors(chunk, slope, average, metal)
    g = group_of(n)
    for j in range(0, n, g):

        def take(ref, part=0):
            rows = pl.ds((part * n + j) * ROWS, g * ROWS)
            return ref[rows, :].reshape(g, ROWS, nz)

        u = take(field, slot)
        residual = source[pl.ds(j, g)] - (here * u + (cond * take(lap) + take(sums)))
        u = u + step * residual
        if last:
            outs[0][pl.ds(j, g)] = u
            outs[1][pl.ds(j, g)] = residual
        else:
            outs[0][pl.ds(j * ROWS, g * ROWS), :] = u.reshape(g * ROWS, nz)
        if double:
            u = take(blended) - step * (cond * take(laps[0]) + take(sums, 1))
            outs[0][pl.ds((n + j) * ROWS, g * ROWS), :] = u.reshape(g * ROWS, nz)


def matrices_kernel(n, count, blocks, me, pairs, entries, out):
    kl, _, listed = pairs.shape
    wide, tall = ceil_to(n, 16), ceil_to(n, 8)
    row = lax.broadcasted_iota(jnp.int32, (tall, listed), 0)
    column = lax.broadcasted_iota(jnp.int32, (wide, listed), 0)
    starts = [lax.rem(me[0] - s + count, count) * n for s in range(count)]
    columns = jnp.concatenate(
        [jnp.where(column < n, start + column, -1) for start in starts], axis=0
    )
    for k in range(kl):
        hits = jnp.where(columns == pairs[k, pl.ds(1, 1), :], 1.0, 0.0).astype(BF16)
        for b in range(blocks):
            rows = jnp.where(row < n, starts[b] + row, -1)
            value = jnp.broadcast_to(entries[pl.ds(k, 1), :], (tall, listed))
            value = jnp.where(rows == pairs[k, pl.ds(0, 1), :], value, 0.0)
            parts = []
            for _ in range(3):
                part = value.astype(BF16)
                value = value - part.astype(F32)
                parts.append(part)
            sums = lax.dot_general(
                jnp.concatenate(parts, axis=0),
                hits,
                (((1,), (1,)), ((), ())),
                preferred_element_type=F32,
            )
            g = sums[:tall] + sums[tall : 2 * tall] + sums[2 * tall :]
            hi = g.astype(BF16)
            lo = (g - hi.astype(F32)).astype(BF16)
            for s in range(count):
                at = slice(s * wide, (s + 1) * wide)
                out[s, pl.ds((b * kl + k) * tall, tall), :] = jnp.concatenate(
                    [hi[:, at], hi[:, at], lo[:, at]], axis=1
                )


def whole(a):
    return pl.BlockSpec(a.shape, lambda i, d=len(a.shape): (0,) * d)


def rows_of(a, chunk):
    return pl.BlockSpec((a.shape[0], ROWS, a.shape[2]), lambda i: (0, chunk, 0))


def estimate(flops, moved):
    return pl.CostEstimate(flops=flops, bytes_accessed=4 * moved, transcendentals=0)


def scratch(n, blocks, kl, nz):
    wide, tall = ceil_to(n, 16), ceil_to(n, 8)
    return [
        pltpu.VMEM((2, 3 * wide, 2 * nz), BF16),
        pltpu.VMEM((2, blocks * kl * tall, 2 * nz), F32),
    ]


def lap_call(n, chunk, prev, cur, nxt, near, far, edge=None, compact=False):
    arrays, slots = zip(prev, cur, nxt, near, far)
    nz = cur[0].shape[1]
    rows = n * ROWS + (0 if edge is None else n)
    return pl.pallas_call(
        functools.partial(lap_kernel, n, chunk, slots, edge, compact),
        out_shape=jax.ShapeDtypeStruct((rows, nz), F32),
        in_specs=[vmem()] * 5,
        out_specs=vmem(),
        compiler_params=params(),
        name="lap",
        cost_estimate=estimate(12 * rows * nz, 6 * rows * nz),
    )(*arrays)


def own_call(n, chunk, blocks, fields, matrices, lap):
    kl, _, nz = fields.shape
    size = n * ROWS * nz
    return pl.pallas_call(
        functools.partial(own_kernel, n, chunk, blocks),
        out_shape=jax.ShapeDtypeStruct((blocks * n * ROWS, nz), F32),
        in_specs=[vmem()] * 3,
        out_specs=vmem(),
        scratch_shapes=scratch(n, blocks, kl, nz),
        compiler_params=params(),
        name="own",
        cost_estimate=estimate(6 * blocks * kl * n * size, 2 * size),
    )(fields, matrices, lap)


def blend_call(n, chunk, shared, field, source):
    nz = field.shape[1]
    size = n * ROWS * nz
    operands = [*shared[1:], field, source]
    return pl.pallas_call(
        functools.partial(blend_kernel, n, chunk),
        grid=(1,),
        out_shape=jax.ShapeDtypeStruct((n * ROWS, nz), F32),
        in_specs=[*(whole(a) for a in operands[:-1]), rows_of(source, chunk)],
        out_specs=pl.BlockSpec((n * ROWS, nz), lambda i: (0, 0)),
        compiler_params=params(),
        name="blend",
        cost_estimate=estimate(4 * size, 3 * size),
    )(*operands)


def final_call(n, chunk, last, shared, matrices, source, field, lap, own, laps, blended, outs):
    nz = source.shape[2]
    double = blended is not None
    blocks = 2 if double else 1
    operands = [*shared, matrices, source, field[0], lap, own, *laps]
    operands += [blended] if double else []
    specs = [rows_of(a, chunk) if a is source else whole(a) for a in operands]
    aliases = {}
    if last:
        shapes = [jax.ShapeDtypeStruct(source.shape, F32)] * 2
        out_specs = [rows_of(source, chunk)] * 2
        if outs:
            aliases = {len(operands) + i: i for i in range(2)}
            operands += list(outs)
            specs += [pl.BlockSpec(memory_space=pl.ANY)] * 2
    else:
        shapes = [jax.ShapeDtypeStruct((blocks * n * ROWS, nz), F32)]
        out_specs = [whole(shapes[0])]
    size = n * ROWS * nz
    kl = shared[0].shape[0]
    return pl.pallas_call(
        functools.partial(final_kernel, n, chunk, field[1], len(laps), last, double),
        grid=(1,),
        out_shape=shapes,
        in_specs=specs,
        out_specs=out_specs,
        scratch_shapes=[
            *scratch(n, blocks, kl, nz),
            pltpu.VMEM((blocks * n * ROWS, nz), F32),
        ],
        input_output_aliases=aliases,
        compiler_params=params(),
        name="final",
        cost_estimate=estimate(6 * blocks * len(laps) * kl * n * size, 6 * size),
    )(*operands)


def coupling(pairs, entries, n, blocks):
    count = lax.axis_size("modes")
    me = lax.axis_index("modes").astype(jnp.int32).reshape(1)
    kl, listed = entries.shape
    wide, tall = ceil_to(n, 16), ceil_to(n, 8)
    shape = (count, blocks * kl * tall, 3 * wide)
    return pl.pallas_call(
        functools.partial(matrices_kernel, n, count, blocks),
        out_shape=jax.ShapeDtypeStruct(shape, BF16),
        in_specs=[pl.BlockSpec(memory_space=pltpu.SMEM), vmem(), vmem()],
        out_specs=vmem(),
        compiler_params=params(),
        name="coupling",
        cost_estimate=estimate(2 * listed * shape[0] * shape[1] * shape[2], 10000),
    )(me, pairs.transpose(0, 2, 1), entries)


def near_swap(x):
    count = lax.axis_size("space")
    return lax.ppermute(x, "space", [(i, i ^ 1) for i in range(count)])


def far_swap(x):
    count = lax.axis_size("space")
    pairs = [(i, (i + (1 if i % 2 else -1)) % count) for i in range(count)]
    return lax.ppermute(x, "space", pairs)


def to_others(x):
    count = lax.axis_size("modes")
    got = []
    for s in range(1, count):
        ring = [(i, (i + s) % count) for i in range(count)]
        got.append(lax.ppermute(x, "modes", ring))
    return got


FINALS = (1, 0, 2, 3)


def doubled(count, devices):
    return count == 4 and devices == 2


def rounds(n, count, u0, source, shared, pairs, entries):
    nz = u0.shape[-1]
    double = doubled(count, lax.axis_size("modes"))
    tail = count - 1
    cut = lambda c: u0[:, c * ROWS : (c + 1) * ROWS].reshape(n * ROWS, nz)
    field = {0: (cut(0), 0)}
    u0, first = lax.optimization_barrier((u0, field[0][0]))
    field[0] = (first, 0)
    for c in range(1, count):
        field[c] = (cut(c), 0)
    matrices = coupling(pairs, entries, n, 2 if double else 1)
    near_whole = near_swap(u0)
    blended = None
    if double:
        blended = blend_call(n, tail, shared, field[tail][0], source)
        (blended,) = to_others(blended)
    outs = ()
    for turn in range(ROUNDS):
        last = turn == ROUNDS - 1
        near, far, parts = {}, {}, {}
        for c in range(count):
            if turn:
                near[c] = (near_swap(field[c][0]), 0)
            else:
                near[c] = (near_whole, 0)
            far[c] = (far_swap(field[c][0]), 0)
        for c in range(count):
            both = double and c == tail
            prev, nxt = field[(c - 1) % count], field[(c + 1) % count]
            edge = None
            if double and last and not both:
                edge = {(tail - 1): ROWS - 1, (tail + 1) % count: 0}.get(c)
            lap = lap_call(n, c, prev, field[c], nxt, near[c], far[c], edge)
            if both and last:
                of_other = lambda a: (a[0], 1)
                handed = [(parts[d % count][3][0], 0) for d in (tail - 1, tail + 1)]
                laps = [
                    lap_call(
                        n,
                        c,
                        handed[0],
                        of_other(field[c]),
                        handed[1],
                        of_other(near[c]),
                        of_other(far[c]),
                        compact=True,
                    )
                ]
            else:
                laps = to_others(lap)
            blocks = 2 if both and not last else 1
            own = own_call(n, c, blocks, shared[0], matrices, lap)
            parts[c] = (field[c], lap, own, laps)
        new = {}
        for c in FINALS if last and double else range(count):
            given = blended if double and c == tail and not last else None
            got = final_call(
                n, c, last, shared, matrices, source, *parts[c], given, outs
            )
            if last:
                outs = got
            else:
                new[c] = (got[0], 0)
        field = new
    return outs


def on_device(
    initial_heat_weights,
    source_weights,
    heat_storage_slope,
    average_diffusivity,
    metal_indicator,
    uncertain_diffusivity_fields,
    basis_index_pairs,
    basis_integral_entries,
):
    n, planes, ny, _ = initial_heat_weights.shape
    assert planes == 1 and ny % ROWS == 0
    u0 = initial_heat_weights[:, 0]
    source = source_weights[:, 0]
    shared = (
        uncertain_diffusivity_fields[:, 0],
        heat_storage_slope[0],
        average_diffusivity[0],
        metal_indicator[0],
    )
    outs = rounds(
        n, ny // ROWS, u0, source, shared, basis_index_pairs, basis_integral_entries
    )
    return (outs[0][:, None], outs[1][:, None])


def solution(mesh):
    placed = (
        P("modes", "space", None, None),
        P("modes", "space", None, None),
        P("space", None, None),
        P("space", None, None),
        P("space", None, None),
        P(None, "space", None, None),
        P(),
        P(),
    )
    return jax.shard_map(
        on_device,
        mesh=mesh,
        in_specs=placed,
        out_specs=(P("modes", "space", None, None), P("modes", "space", None, None)),
        check_vma=False,
    )
```

```python
import functools

import jax
import jax.numpy as jnp
from jax import lax
from jax.experimental import pallas as pl
from jax.experimental.pallas import tpu as pltpu
from jax.sharding import PartitionSpec as P


ROUNDS = 2
RELAXATION = 0.8
ROWS = 8
F32, BF16 = jnp.float32, jnp.bfloat16


def ceil_to(value, unit):
    return -(-value // unit) * unit


def group_of(n):
    return max(g for g in range(1, 7) if n % g == 0)


def params():
    return pltpu.CompilerParams(vmem_limit_bytes=6 * 1024 * 1024)


def vmem():
    return pl.BlockSpec(memory_space=pltpu.VMEM)


def cell_factors(chunk, slope, average, metal):
    at = pl.ds(chunk * ROWS, ROWS)
    here = slope[at, :]
    cond = average[at, :] * (1.0 + 3.0 * metal[at, :].astype(F32))
    return here, cond, RELAXATION * (1.0 / (here + 6.0 * cond))


def lap_kernel(n, chunk, slots, edge, compact, prev, cur, nxt, near, far, out):
    nz = cur.shape[1]
    g = group_of(n)
    row = lax.broadcasted_iota(jnp.int32, (g, ROWS, nz), 1)
    for j in range(0, n, g):

        def take(ref, slot):
            return ref[pl.ds((slot * n + j) * ROWS, g * ROWS), :].reshape(g, ROWS, nz)

        def handed(ref, at):
            rows = [ref[pl.ds(at + j + i, 1), :] for i in range(g)]
            return jnp.stack([jnp.broadcast_to(r, (ROWS, nz)) for r in rows])

        x = take(cur, slots[1])
        if compact:
            before, after = handed(prev, n * ROWS), handed(nxt, n * ROWS + ceil_to(n, 8))
        else:
            before = pltpu.roll(take(prev, slots[0]), 1, 1)
            after = pltpu.roll(take(nxt, slots[2]), ROWS - 1, 1)
        if len(near.shape) == 3:
            inside = near[pl.ds(j, g), pl.ds(chunk * ROWS, ROWS), :]
        else:
            inside = take(near, slots[3])
        up = jnp.where(row == 0, before, pltpu.roll(x, 1, 1))
        down = jnp.where(row == ROWS - 1, after, pltpu.roll(x, ROWS - 1, 1))
        sides = pltpu.roll(x, 1, 2) + pltpu.roll(x, nz - 1, 2)
        beside = (up + down) + sides + (inside + take(far, slots[4]))
        out[pl.ds(j * ROWS, g * ROWS), :] = (6.0 * x - beside).reshape(g * ROWS, nz)
    if edge:
        for i, (ref, slot, y) in enumerate(((nxt, slots[2], ROWS - 1), (prev, slots[0], 0))):
            got = ref[pl.ds(slot * n * ROWS + y, n, stride=ROWS), :]
            out[pl.ds(n * ROWS + i * ceil_to(n, 8), n), :] = got


def couple(n, chunk, blocks, fields, matrix, lap, rhs, mixed, emit):
    nz = lap.shape[1]
    kl = fields.shape[0]
    wide, tall = ceil_to(n, 16), ceil_to(n, 8)
    used = pl.ds(0, blocks * kl * tall)
    for pair in range(ROWS // 2):
        slot = pair % 2
        for half in range(2):
            v = lap[pl.ds(2 * pair + half, n, stride=ROWS), :]
            hi = v.astype(BF16)
            lo = (v - hi.astype(F32)).astype(BF16)
            cols = pl.ds(half * nz, nz)
            rhs[slot, pl.ds(0, n), cols] = hi
            rhs[slot, pl.ds(wide, n), cols] = lo
            rhs[slot, pl.ds(2 * wide, n), cols] = hi
        mixed[slot] = jnp.dot(matrix[used, :], rhs[slot], preferred_element_type=F32)
        for half in range(2):
            y = 2 * pair + half
            cols = pl.ds(half * nz, nz)
            for b in range(blocks):
                total = None
                for k in range(kl):
                    field = fields[k, pl.ds(chunk * ROWS + y, 1), :]
                    at = pl.ds((b * kl + k) * tall, n)
                    term = field * mixed[slot, at, cols]
                    total = term if total is None else total + term
                emit(y, b, total)


def clear_rhs(n, rhs):
    if ceil_to(n, 16) != n:
        rhs[...] = jnp.zeros_like(rhs)


def own_kernel(n, chunk, blocks, fields, matrices, lap, out, rhs, mixed):
    clear_rhs(n, rhs)

    def emit(y, b, total):
        out[pl.ds(b * n * ROWS + y, n, stride=ROWS), :] = total

    couple(n, chunk, blocks, fields, matrices.at[0], lap, rhs, mixed, emit)


def blend_kernel(n, chunk, slope, average, metal, field, source, out):
    nz = field.shape[1]
    here, _, step = cell_factors(chunk, slope, average, metal)
    g = group_of(n)
    for j in range(0, n, g):
        rows = pl.ds(j * ROWS, g * ROWS)
        u = field[rows, :].reshape(g, ROWS, nz)
        v = u + step * (source[pl.ds(j, g)] - here * u)
        out[rows, :] = v.reshape(g * ROWS, nz)


def final_kernel(n, entries, last, double, *refs):
    fields, slope, average, metal, matrices, source = refs[:6]
    refs = refs[6:]
    groups = []
    for chunk, slot, has_own, others in entries:
        size = 2 + has_own + others
        groups.append((chunk, slot, has_own, refs[:size]))
        refs = refs[size:]
    blended, refs = (refs[0], refs[1:]) if double else (None, refs)
    outs, (rhs, mixed, sums) = refs[:-3], refs[-3:]
    outs = outs[2:] if len(outs) == 4 else outs
    clear_rhs(n, rhs)
    g = group_of(n)
    for index, (chunk, slot, has_own, (field, lap, *laps)) in enumerate(groups):
        nz = lap.shape[1]
        base = laps[0] if has_own else None
        laps = laps[1:] if has_own else [lap, *laps]
        for other, received in enumerate(laps):

            def emit(y, b, total):
                at = pl.ds(b * n * ROWS + y, n, stride=ROWS)
                sums[at, :] = total if base is None else base[at, :] + total

            couple(
                n,
                chunk,
                2 if double else 1,
                fields,
                matrices.at[other + has_own],
                received,
                rhs,
                mixed,
                emit,
            )
            base = sums
        here, cond, step = cell_factors(chunk, slope, average, metal)
        rows_here = pl.ds(index * ROWS, ROWS)
        for j in range(0, n, g):

            def take(ref, part=0):
                rows = pl.ds((part * n + j) * ROWS, g * ROWS)
                return ref[rows, :].reshape(g, ROWS, nz)

            u = take(field, slot)
            rest = here * u + (cond * take(lap) + take(sums))
            residual = source[pl.ds(j, g), rows_here, :] - rest
            u = u + step * residual
            if last:
                outs[0][pl.ds(j, g), rows_here, :] = u
                outs[1][pl.ds(j, g), rows_here, :] = residual
            else:
                outs[0][pl.ds(j * ROWS, g * ROWS), :] = u.reshape(g * ROWS, nz)
            if double:
                u = take(blended) - step * (cond * take(laps[0]) + take(sums, 1))
                outs[0][pl.ds((n + j) * ROWS, g * ROWS), :] = u.reshape(g * ROWS, nz)


def matrices_kernel(n, count, blocks, me, pairs, entries, out):
    kl, _, listed = pairs.shape
    wide, tall = ceil_to(n, 16), ceil_to(n, 8)
    row = lax.broadcasted_iota(jnp.int32, (tall, listed), 0)
    column = lax.broadcasted_iota(jnp.int32, (wide, listed), 0)
    starts = [lax.rem(me[0] - s + count, count) * n for s in range(count)]
    columns = jnp.concatenate(
        [jnp.where(column < n, start + column, -1) for start in starts], axis=0
    )
    for k in range(kl):
        hits = jnp.where(columns == pairs[k, pl.ds(1, 1), :], 1.0, 0.0).astype(BF16)
        for b in range(blocks):
            rows = jnp.where(row < n, starts[b] + row, -1)
            value = jnp.broadcast_to(entries[pl.ds(k, 1), :], (tall, listed))
            value = jnp.where(rows == pairs[k, pl.ds(0, 1), :], value, 0.0)
            parts = []
            for _ in range(3):
                part = value.astype(BF16)
                value = value - part.astype(F32)
                parts.append(part)
            sums = lax.dot_general(
                jnp.concatenate(parts, axis=0),
                hits,
                (((1,), (1,)), ((), ())),
                preferred_element_type=F32,
            )
            g = sums[:tall] + sums[tall : 2 * tall] + sums[2 * tall :]
            hi = g.astype(BF16)
            lo = (g - hi.astype(F32)).astype(BF16)
            for s in range(count):
                at = slice(s * wide, (s + 1) * wide)
                out[s, pl.ds((b * kl + k) * tall, tall), :] = jnp.concatenate(
                    [hi[:, at], hi[:, at], lo[:, at]], axis=1
                )


def whole(a):
    return pl.BlockSpec(a.shape, lambda i, d=len(a.shape): (0,) * d)


def rows_of(a, chunk):
    return pl.BlockSpec((a.shape[0], ROWS, a.shape[2]), lambda i: (0, chunk, 0))


def estimate(flops, moved):
    return pl.CostEstimate(flops=flops, bytes_accessed=4 * moved, transcendentals=0)


def scratch(n, blocks, kl, nz):
    wide, tall = ceil_to(n, 16), ceil_to(n, 8)
    return [
        pltpu.VMEM((2, 3 * wide, 2 * nz), BF16),
        pltpu.VMEM((2, blocks * kl * tall, 2 * nz), F32),
    ]


def lap_call(n, chunk, prev, cur, nxt, near, far, edge=False, compact=False):
    arrays, slots = zip(prev, cur, nxt, near, far)
    nz = cur[0].shape[1]
    rows = n * ROWS + (2 * ceil_to(n, 8) if edge else 0)
    return pl.pallas_call(
        functools.partial(lap_kernel, n, chunk, slots, edge, compact),
        out_shape=jax.ShapeDtypeStruct((rows, nz), F32),
        in_specs=[vmem()] * 5,
        out_specs=vmem(),
        compiler_params=params(),
        name="lap",
        cost_estimate=estimate(12 * rows * nz, 6 * rows * nz),
    )(*arrays)


def own_call(n, chunk, blocks, fields, matrices, lap):
    kl, _, nz = fields.shape
    size = n * ROWS * nz
    return pl.pallas_call(
        functools.partial(own_kernel, n, chunk, blocks),
        out_shape=jax.ShapeDtypeStruct((blocks * n * ROWS, nz), F32),
        in_specs=[vmem()] * 3,
        out_specs=vmem(),
        scratch_shapes=scratch(n, blocks, kl, nz),
        compiler_params=params(),
        name="own",
        cost_estimate=estimate(6 * blocks * kl * n * size, 2 * size),
    )(fields, matrices, lap)


def blend_call(n, chunk, shared, field, source):
    nz = field.shape[1]
    size = n * ROWS * nz
    operands = [*shared[1:], field, source]
    return pl.pallas_call(
        functools.partial(blend_kernel, n, chunk),
        grid=(1,),
        out_shape=jax.ShapeDtypeStruct((n * ROWS, nz), F32),
        in_specs=[*(whole(a) for a in operands[:-1]), rows_of(source, chunk)],
        out_specs=pl.BlockSpec((n * ROWS, nz), lambda i: (0, 0)),
        compiler_params=params(),
        name="blend",
        cost_estimate=estimate(4 * size, 3 * size),
    )(*operands)


def final_call(n, chunks, last, shared, matrices, source, parts, blended, outs):
    nz = source.shape[2]
    double = blended is not None
    blocks = 2 if double else 1
    block = pl.BlockSpec(
        (n, len(chunks) * ROWS, nz), lambda i: (0, chunks[0] // len(chunks), 0)
    )
    operands, entries = [*shared, matrices, source], []
    for chunk, (field, lap, own, laps) in zip(chunks, parts):
        entries.append((chunk, field[1], own is not None, len(laps)))
        operands += [field[0], lap, *([] if own is None else [own]), *laps]
    operands += [blended] if double else []
    specs = [block if a is source else whole(a) for a in operands]
    aliases = {}
    if last:
        shapes = [jax.ShapeDtypeStruct(source.shape, F32)] * 2
        out_specs = [block] * 2
        if outs:
            aliases = {len(operands) + i: i for i in range(2)}
            operands += list(outs)
            specs += [pl.BlockSpec(memory_space=pl.ANY)] * 2
    else:
        shapes = [jax.ShapeDtypeStruct((blocks * n * ROWS, nz), F32)]
        out_specs = [whole(shapes[0])]
    size = len(chunks) * n * ROWS * nz
    kl = shared[0].shape[0]
    return pl.pallas_call(
        functools.partial(final_kernel, n, tuple(entries), last, double),
        grid=(1,),
        out_shape=shapes,
        in_specs=specs,
        out_specs=out_specs,
        scratch_shapes=[
            *scratch(n, blocks, kl, nz),
            pltpu.VMEM((blocks * n * ROWS, nz), F32),
        ],
        input_output_aliases=aliases,
        compiler_params=params(),
        name="final",
        cost_estimate=estimate(6 * blocks * kl * n * size, 6 * size),
    )(*operands)


def coupling(pairs, entries, n, blocks):
    count = lax.axis_size("modes")
    me = lax.axis_index("modes").astype(jnp.int32).reshape(1)
    kl, listed = entries.shape
    wide, tall = ceil_to(n, 16), ceil_to(n, 8)
    shape = (count, blocks * kl * tall, 3 * wide)
    return pl.pallas_call(
        functools.partial(matrices_kernel, n, count, blocks),
        out_shape=jax.ShapeDtypeStruct(shape, BF16),
        in_specs=[pl.BlockSpec(memory_space=pltpu.SMEM), vmem(), vmem()],
        out_specs=vmem(),
        compiler_params=params(),
        name="coupling",
        cost_estimate=estimate(2 * listed * shape[0] * shape[1] * shape[2], 10000),
    )(me, pairs.transpose(0, 2, 1), entries)


def near_swap(x):
    count = lax.axis_size("space")
    return lax.ppermute(x, "space", [(i, i ^ 1) for i in range(count)])


def far_swap(x):
    count = lax.axis_size("space")
    pairs = [(i, (i + (1 if i % 2 else -1)) % count) for i in range(count)]
    return lax.ppermute(x, "space", pairs)


def to_others(x):
    count = lax.axis_size("modes")
    got = []
    for s in range(1, count):
        ring = [(i, (i + s) % count) for i in range(count)]
        got.append(lax.ppermute(x, "modes", ring))
    return got


FINALS = ((1,), (0,), (2, 3))


def doubled(count, devices):
    return count == 4 and devices == 2


def rounds(n, count, u0, source, shared, pairs, entries):
    nz = u0.shape[-1]
    double = doubled(count, lax.axis_size("modes"))
    tail = count - 1
    cut = lambda c: u0[:, c * ROWS : (c + 1) * ROWS].reshape(n * ROWS, nz)
    field = {0: (cut(0), 0)}
    u0, first = lax.optimization_barrier((u0, field[0][0]))
    field[0] = (first, 0)
    for c in range(1, count):
        field[c] = (cut(c), 0)
    matrices = coupling(pairs, entries, n, 2 if double else 1)
    near_whole = near_swap(u0)
    blended = None
    if double:
        blended = blend_call(n, tail, shared, field[tail][0], source)
        (blended,) = to_others(blended)
    outs = ()
    for turn in range(ROUNDS):
        last = turn == ROUNDS - 1
        near, far, parts = {}, {}, {}
        for c in range(count):
            if turn:
                near[c] = (near_swap(field[c][0]), 0)
            else:
                near[c] = (near_whole, 0)
            far[c] = (far_swap(field[c][0]), 0)
        for c in range(count):
            both = double and c == tail
            prev, nxt = field[(c - 1) % count], field[(c + 1) % count]
            edge = double and last and c == tail - 2
            lap = lap_call(n, c, prev, field[c], nxt, near[c], far[c], edge)
            if both and last:
                of_other = lambda a: (a[0], 1)
                handed = (parts[tail - 2][3][0], 0)
                laps = [
                    lap_call(
                        n,
                        c,
                        handed,
                        of_other(field[c]),
                        handed,
                        of_other(near[c]),
                        of_other(far[c]),
                        compact=True,
                    )
                ]
            else:
                laps = to_others(lap)
            own = None
            if not (both and last):
                blocks = 2 if both else 1
                own = own_call(n, c, blocks, shared[0], matrices, lap)
            parts[c] = (field[c], lap, own, laps)
        new = {}
        for chunks in FINALS if last and double else [(c,) for c in range(count)]:
            c = chunks[0]
            given = blended if double and c == tail and not last else None
            got = final_call(
                n,
                chunks,
                last,
                shared,
                matrices,
                source,
                [parts[d] for d in chunks],
                given,
                outs,
            )
            if last:
                outs = got
            else:
                new[c] = (got[0], 0)
        field = new
    return outs


def on_device(
    initial_heat_weights,
    source_weights,
    heat_storage_slope,
    average_diffusivity,
    metal_indicator,
    uncertain_diffusivity_fields,
    basis_index_pairs,
    basis_integral_entries,
):
    n, planes, ny, _ = initial_heat_weights.shape
    assert planes == 1 and ny % ROWS == 0
    u0 = initial_heat_weights[:, 0]
    source = source_weights[:, 0]
    shared = (
        uncertain_diffusivity_fields[:, 0],
        heat_storage_slope[0],
        average_diffusivity[0],
        metal_indicator[0],
    )
    outs = rounds(
        n, ny // ROWS, u0, source, shared, basis_index_pairs, basis_integral_entries
    )
    return (outs[0][:, None], outs[1][:, None])


def solution(mesh):
    placed = (
        P("modes", "space", None, None),
        P("modes", "space", None, None),
        P("space", None, None),
        P("space", None, None),
        P("space", None, None),
        P(None, "space", None, None),
        P(),
        P(),
    )
    return jax.shard_map(
        on_device,
        mesh=mesh,
        in_specs=placed,
        out_specs=(P("modes", "space", None, None), P("modes", "space", None, None)),
        check_vma=False,
    )
```

```python
import functools

import jax
import jax.numpy as jnp
from jax import lax
from jax.experimental import pallas as pl
from jax.experimental.pallas import tpu as pltpu
from jax.sharding import PartitionSpec as P


ROUNDS = 2
RELAXATION = 0.8
ROWS = 8
F32, BF16 = jnp.float32, jnp.bfloat16


def ceil_to(value, unit):
    return -(-value // unit) * unit


def group_of(n):
    return max(g for g in range(1, 7) if n % g == 0)


def params():
    return pltpu.CompilerParams(vmem_limit_bytes=6 * 1024 * 1024)


def vmem():
    return pl.BlockSpec(memory_space=pltpu.VMEM)


def cell_factors(chunk, slope, average, metal):
    at = pl.ds(chunk * ROWS, ROWS)
    here = slope[at, :]
    cond = average[at, :] * (1.0 + 3.0 * metal[at, :].astype(F32))
    return here, cond, RELAXATION * (1.0 / (here + 6.0 * cond))


def lap_kernel(n, chunk, slots, edge, compact, prev, cur, nxt, near, far, out):
    nz = cur.shape[1]
    g = group_of(n)
    row = lax.broadcasted_iota(jnp.int32, (g, ROWS, nz), 1)
    for j in range(0, n, g):

        def take(ref, slot):
            return ref[pl.ds((slot * n + j) * ROWS, g * ROWS), :].reshape(g, ROWS, nz)

        def handed(ref, at):
            rows = [ref[pl.ds(at + j + i, 1), :] for i in range(g)]
            return jnp.stack([jnp.broadcast_to(r, (ROWS, nz)) for r in rows])

        x = take(cur, slots[1])
        if compact:
            before, after = handed(prev, n * ROWS), handed(nxt, n * ROWS + ceil_to(n, 8))
        else:
            before = pltpu.roll(take(prev, slots[0]), 1, 1)
            after = pltpu.roll(take(nxt, slots[2]), ROWS - 1, 1)
        if len(near.shape) == 3:
            inside = near[pl.ds(j, g), pl.ds(chunk * ROWS, ROWS), :]
        else:
            inside = take(near, slots[3])
        up = jnp.where(row == 0, before, pltpu.roll(x, 1, 1))
        down = jnp.where(row == ROWS - 1, after, pltpu.roll(x, ROWS - 1, 1))
        sides = pltpu.roll(x, 1, 2) + pltpu.roll(x, nz - 1, 2)
        beside = (up + down) + sides + (inside + take(far, slots[4]))
        out[pl.ds(j * ROWS, g * ROWS), :] = (6.0 * x - beside).reshape(g * ROWS, nz)
    if edge:
        for i, (ref, slot, y) in enumerate(((nxt, slots[2], ROWS - 1), (prev, slots[0], 0))):
            got = ref[pl.ds(slot * n * ROWS + y, n, stride=ROWS), :]
            out[pl.ds(n * ROWS + i * ceil_to(n, 8), n), :] = got


def couple(n, chunk, blocks, fields, matrix, lap, rhs, mixed, emit):
    nz = lap.shape[1]
    kl = fields.shape[0]
    wide, tall = ceil_to(n, 16), ceil_to(n, 8)
    used = pl.ds(0, blocks * kl * tall)
    for pair in range(ROWS // 2):
        slot = pair % 2
        for half in range(2):
            v = lap[pl.ds(2 * pair + half, n, stride=ROWS), :]
            hi = v.astype(BF16)
            lo = (v - hi.astype(F32)).astype(BF16)
            cols = pl.ds(half * nz, nz)
            rhs[slot, pl.ds(0, n), cols] = hi
            rhs[slot, pl.ds(wide, n), cols] = lo
            rhs[slot, pl.ds(2 * wide, n), cols] = hi
        mixed[slot] = jnp.dot(matrix[used, :], rhs[slot], preferred_element_type=F32)
        for half in range(2):
            y = 2 * pair + half
            cols = pl.ds(half * nz, nz)
            for b in range(blocks):
                total = None
                for k in range(kl):
                    field = fields[k, pl.ds(chunk * ROWS + y, 1), :]
                    at = pl.ds((b * kl + k) * tall, n)
                    term = field * mixed[slot, at, cols]
                    total = term if total is None else total + term
                emit(y, b, total)


def clear_rhs(n, rhs):
    if ceil_to(n, 16) != n:
        rhs[...] = jnp.zeros_like(rhs)


def own_kernel(n, chunk, blocks, fields, matrices, lap, out, rhs, mixed):
    clear_rhs(n, rhs)

    def emit(y, b, total):
        out[pl.ds(b * n * ROWS + y, n, stride=ROWS), :] = total

    couple(n, chunk, blocks, fields, matrices.at[0], lap, rhs, mixed, emit)


def final_kernel(n, entries, last, double, *refs):
    fields, slope, average, metal, matrices, source = refs[:6]
    refs = refs[6:]
    groups = []
    for chunk, slot, has_own, others in entries:
        size = 2 + has_own + others
        groups.append((chunk, slot, has_own, refs[:size]))
        refs = refs[size:]
    blended, refs = (refs[0], refs[1:]) if double else (None, refs)
    outs, (rhs, mixed, sums) = refs[:-3], refs[-3:]
    outs = outs[2:] if len(outs) == 4 else outs
    clear_rhs(n, rhs)
    g = group_of(n)
    for index, (chunk, slot, has_own, (field, lap, *laps)) in enumerate(groups):
        nz = lap.shape[1]
        base = laps[0] if has_own else None
        laps = laps[1:] if has_own else [lap, *laps]
        for other, received in enumerate(laps):

            def emit(y, b, total):
                at = pl.ds(b * n * ROWS + y, n, stride=ROWS)
                sums[at, :] = total if base is None else base[at, :] + total

            couple(
                n,
                chunk,
                2 if double else 1,
                fields,
                matrices.at[other + has_own],
                received,
                rhs,
                mixed,
                emit,
            )
            base = sums
        here, cond, step = cell_factors(chunk, slope, average, metal)
        rows_here = pl.ds(index * ROWS, ROWS)
        for j in range(0, n, g):

            def take(ref, part=0):
                rows = pl.ds((part * n + j) * ROWS, g * ROWS)
                return ref[rows, :].reshape(g, ROWS, nz)

            u = take(field, slot)
            rest = here * u + (cond * take(lap) + take(sums))
            residual = source[pl.ds(j, g), rows_here, :] - rest
            u = u + step * residual
            if last:
                outs[0][pl.ds(j, g), rows_here, :] = u
                outs[1][pl.ds(j, g), rows_here, :] = residual
            else:
                outs[0][pl.ds(j * ROWS, g * ROWS), :] = u.reshape(g * ROWS, nz)
            if double:
                u = take(blended) - step * (cond * take(laps[0]) + take(sums, 1))
                outs[0][pl.ds((n + j) * ROWS, g * ROWS), :] = u.reshape(g * ROWS, nz)


def matrices_kernel(n, count, blocks, me, pairs, entries, out):
    kl, _, listed = pairs.shape
    wide, tall = ceil_to(n, 16), ceil_to(n, 8)
    row = lax.broadcasted_iota(jnp.int32, (tall, listed), 0)
    column = lax.broadcasted_iota(jnp.int32, (wide, listed), 0)
    starts = [lax.rem(me[0] - s + count, count) * n for s in range(count)]
    columns = jnp.concatenate(
        [jnp.where(column < n, start + column, -1) for start in starts], axis=0
    )
    for k in range(kl):
        hits = jnp.where(columns == pairs[k, pl.ds(1, 1), :], 1.0, 0.0).astype(BF16)
        for b in range(blocks):
            rows = jnp.where(row < n, starts[b] + row, -1)
            value = jnp.broadcast_to(entries[pl.ds(k, 1), :], (tall, listed))
            value = jnp.where(rows == pairs[k, pl.ds(0, 1), :], value, 0.0)
            parts = []
            for _ in range(3):
                part = value.astype(BF16)
                value = value - part.astype(F32)
                parts.append(part)
            sums = lax.dot_general(
                jnp.concatenate(parts, axis=0),
                hits,
                (((1,), (1,)), ((), ())),
                preferred_element_type=F32,
            )
            g = sums[:tall] + sums[tall : 2 * tall] + sums[2 * tall :]
            hi = g.astype(BF16)
            lo = (g - hi.astype(F32)).astype(BF16)
            for s in range(count):
                at = slice(s * wide, (s + 1) * wide)
                out[s, pl.ds((b * kl + k) * tall, tall), :] = jnp.concatenate(
                    [hi[:, at], hi[:, at], lo[:, at]], axis=1
                )


def whole(a):
    return pl.BlockSpec(a.shape, lambda i, d=len(a.shape): (0,) * d)


def estimate(flops, moved):
    return pl.CostEstimate(flops=flops, bytes_accessed=4 * moved, transcendentals=0)


def scratch(n, blocks, kl, nz):
    wide, tall = ceil_to(n, 16), ceil_to(n, 8)
    return [
        pltpu.VMEM((2, 3 * wide, 2 * nz), BF16),
        pltpu.VMEM((2, blocks * kl * tall, 2 * nz), F32),
    ]


def lap_call(n, chunk, prev, cur, nxt, near, far, edge=False, compact=False):
    arrays, slots = zip(prev, cur, nxt, near, far)
    nz = cur[0].shape[1]
    rows = n * ROWS + (2 * ceil_to(n, 8) if edge else 0)
    return pl.pallas_call(
        functools.partial(lap_kernel, n, chunk, slots, edge, compact),
        out_shape=jax.ShapeDtypeStruct((rows, nz), F32),
        in_specs=[vmem()] * 5,
        out_specs=vmem(),
        compiler_params=params(),
        name="lap",
        cost_estimate=estimate(12 * rows * nz, 6 * rows * nz),
    )(*arrays)


def own_call(n, chunk, blocks, fields, matrices, lap):
    kl, _, nz = fields.shape
    size = n * ROWS * nz
    return pl.pallas_call(
        functools.partial(own_kernel, n, chunk, blocks),
        out_shape=jax.ShapeDtypeStruct((blocks * n * ROWS, nz), F32),
        in_specs=[vmem()] * 3,
        out_specs=vmem(),
        scratch_shapes=scratch(n, blocks, kl, nz),
        compiler_params=params(),
        name="own",
        cost_estimate=estimate(6 * blocks * kl * n * size, 2 * size),
    )(fields, matrices, lap)


def final_call(n, chunks, last, shared, matrices, source, parts, blended, outs):
    nz = source.shape[2]
    double = blended is not None
    blocks = 2 if double else 1
    block = pl.BlockSpec(
        (n, len(chunks) * ROWS, nz), lambda i: (0, chunks[0] // len(chunks), 0)
    )
    operands, entries = [*shared, matrices, source], []
    for chunk, (field, lap, own, laps) in zip(chunks, parts):
        entries.append((chunk, field[1], own is not None, len(laps)))
        operands += [field[0], lap, *([] if own is None else [own]), *laps]
    operands += [blended] if double else []
    specs = [block if a is source else whole(a) for a in operands]
    aliases = {}
    if last:
        shapes = [jax.ShapeDtypeStruct(source.shape, F32)] * 2
        out_specs = [block] * 2
        if outs:
            aliases = {len(operands) + i: i for i in range(2)}
            operands += list(outs)
            specs += [pl.BlockSpec(memory_space=pl.ANY)] * 2
    else:
        shapes = [jax.ShapeDtypeStruct((blocks * n * ROWS, nz), F32)]
        out_specs = [whole(shapes[0])]
    size = len(chunks) * n * ROWS * nz
    kl = shared[0].shape[0]
    return pl.pallas_call(
        functools.partial(final_kernel, n, tuple(entries), last, double),
        grid=(1,),
        out_shape=shapes,
        in_specs=specs,
        out_specs=out_specs,
        scratch_shapes=[
            *scratch(n, blocks, kl, nz),
            pltpu.VMEM((blocks * n * ROWS, nz), F32),
        ],
        input_output_aliases=aliases,
        compiler_params=params(),
        name="final",
        cost_estimate=estimate(6 * blocks * kl * n * size, 6 * size),
    )(*operands)


def coupling(pairs, entries, n, blocks):
    count = lax.axis_size("modes")
    me = lax.axis_index("modes").astype(jnp.int32).reshape(1)
    kl, listed = entries.shape
    wide, tall = ceil_to(n, 16), ceil_to(n, 8)
    shape = (count, blocks * kl * tall, 3 * wide)
    return pl.pallas_call(
        functools.partial(matrices_kernel, n, count, blocks),
        out_shape=jax.ShapeDtypeStruct(shape, BF16),
        in_specs=[pl.BlockSpec(memory_space=pltpu.SMEM), vmem(), vmem()],
        out_specs=vmem(),
        compiler_params=params(),
        name="coupling",
        cost_estimate=estimate(2 * listed * shape[0] * shape[1] * shape[2], 10000),
    )(me, pairs.transpose(0, 2, 1), entries)


def near_swap(x):
    count = lax.axis_size("space")
    return lax.ppermute(x, "space", [(i, i ^ 1) for i in range(count)])


def far_swap(x):
    count = lax.axis_size("space")
    pairs = [(i, (i + (1 if i % 2 else -1)) % count) for i in range(count)]
    return lax.ppermute(x, "space", pairs)


def to_others(x):
    count = lax.axis_size("modes")
    got = []
    for s in range(1, count):
        ring = [(i, (i + s) % count) for i in range(count)]
        got.append(lax.ppermute(x, "modes", ring))
    return got


FINALS = ((1,), (0,), (2, 3))


def doubled(count, devices):
    return count == 4 and devices == 2


def rounds(n, count, u0, source, shared, pairs, entries):
    nz = u0.shape[-1]
    double = doubled(count, lax.axis_size("modes"))
    tail = count - 1
    cut = lambda c: u0[:, c * ROWS : (c + 1) * ROWS].reshape(n * ROWS, nz)
    field = {0: (cut(0), 0)}
    u0, first = lax.optimization_barrier((u0, field[0][0]))
    field[0] = (first, 0)
    for c in range(1, count):
        field[c] = (cut(c), 0)
    matrices = coupling(pairs, entries, n, 2 if double else 1)
    near_whole = near_swap(u0)
    blended = None
    if double:
        _, slope, average, metal = (a[..., tail * ROWS : count * ROWS, :] for a in shared)
        step = RELAXATION / (slope + 6.0 * average * (1.0 + 3.0 * metal.astype(F32)))
        u = u0[:, tail * ROWS : count * ROWS]
        v = u + step * (source[:, tail * ROWS : count * ROWS] - slope * u)
        blended = v.reshape(n * ROWS, nz)
        (blended,) = to_others(blended)
    outs = ()
    for turn in range(ROUNDS):
        last = turn == ROUNDS - 1
        near, far, parts = {}, {}, {}
        for c in range(count):
            if turn:
                near[c] = (near_swap(field[c][0]), 0)
            else:
                near[c] = (near_whole, 0)
            far[c] = (far_swap(field[c][0]), 0)
        for c in range(count):
            both = double and c == tail
            prev, nxt = field[(c - 1) % count], field[(c + 1) % count]
            edge = double and last and c == tail - 2
            lap = lap_call(n, c, prev, field[c], nxt, near[c], far[c], edge)
            if both and last:
                of_other = lambda a: (a[0], 1)
                handed = (parts[tail - 2][3][0], 0)
                laps = [
                    lap_call(
                        n,
                        c,
                        handed,
                        of_other(field[c]),
                        handed,
                        of_other(near[c]),
                        of_other(far[c]),
                        compact=True,
                    )
                ]
            else:
                laps = to_others(lap)
            own = None
            if not (both and last):
                blocks = 2 if both else 1
                own = own_call(n, c, blocks, shared[0], matrices, lap)
            parts[c] = (field[c], lap, own, laps)
        new = {}
        for chunks in FINALS if last and double else [(c,) for c in range(count)]:
            c = chunks[0]
            given = blended if double and c == tail and not last else None
            got = final_call(
                n,
                chunks,
                last,
                shared,
                matrices,
                source,
                [parts[d] for d in chunks],
                given,
                outs,
            )
            if last:
                outs = got
            else:
                new[c] = (got[0], 0)
        field = new
    return outs


def on_device(
    initial_heat_weights,
    source_weights,
    heat_storage_slope,
    average_diffusivity,
    metal_indicator,
    uncertain_diffusivity_fields,
    basis_index_pairs,
    basis_integral_entries,
):
    n, planes, ny, _ = initial_heat_weights.shape
    assert planes == 1 and ny % ROWS == 0
    u0 = initial_heat_weights[:, 0]
    source = source_weights[:, 0]
    shared = (
        uncertain_diffusivity_fields[:, 0],
        heat_storage_slope[0],
        average_diffusivity[0],
        metal_indicator[0],
    )
    outs = rounds(
        n, ny // ROWS, u0, source, shared, basis_index_pairs, basis_integral_entries
    )
    return (outs[0][:, None], outs[1][:, None])


def solution(mesh):
    placed = (
        P("modes", "space", None, None),
        P("modes", "space", None, None),
        P("space", None, None),
        P("space", None, None),
        P("space", None, None),
        P(None, "space", None, None),
        P(),
        P(),
    )
    return jax.shard_map(
        on_device,
        mesh=mesh,
        in_specs=placed,
        out_specs=(P("modes", "space", None, None), P("modes", "space", None, None)),
        check_vma=False,
    )
```

```python
import functools

import jax
import jax.numpy as jnp
from jax import lax
from jax.experimental import pallas as pl
from jax.experimental.pallas import tpu as pltpu
from jax.sharding import PartitionSpec as P


ROUNDS = 2
RELAXATION = 0.8
ROWS = 8
TOGETHER = 8
SLOTS = min(2, ROWS // TOGETHER)
F32, BF16 = jnp.float32, jnp.bfloat16


def ceil_to(value, unit):
    return -(-value // unit) * unit


def group_of(n):
    return max(g for g in range(1, 7) if n % g == 0)


def params():
    return pltpu.CompilerParams(vmem_limit_bytes=6 * 1024 * 1024)


def vmem():
    return pl.BlockSpec(memory_space=pltpu.VMEM)


def cell_factors(chunk, slope, average, metal):
    at = pl.ds(chunk * ROWS, ROWS)
    here = slope[at, :]
    cond = average[at, :] * (1.0 + 3.0 * metal[at, :].astype(F32))
    return here, cond, RELAXATION * (1.0 / (here + 6.0 * cond))


def lap_kernel(n, chunk, slots, edge, compact, prev, cur, nxt, near, far, out):
    nz = cur.shape[1]
    g = group_of(n)
    row = lax.broadcasted_iota(jnp.int32, (g, ROWS, nz), 1)
    for j in range(0, n, g):

        def take(ref, slot):
            return ref[pl.ds((slot * n + j) * ROWS, g * ROWS), :].reshape(g, ROWS, nz)

        def handed(ref, at):
            rows = [ref[pl.ds(at + j + i, 1), :] for i in range(g)]
            return jnp.stack([jnp.broadcast_to(r, (ROWS, nz)) for r in rows])

        x = take(cur, slots[1])
        if compact:
            before, after = handed(prev, n * ROWS), handed(nxt, n * ROWS + ceil_to(n, 8))
        else:
            before = pltpu.roll(take(prev, slots[0]), 1, 1)
            after = pltpu.roll(take(nxt, slots[2]), ROWS - 1, 1)
        if len(near.shape) == 3:
            inside = near[pl.ds(j, g), pl.ds(chunk * ROWS, ROWS), :]
        else:
            inside = take(near, slots[3])
        up = jnp.where(row == 0, before, pltpu.roll(x, 1, 1))
        down = jnp.where(row == ROWS - 1, after, pltpu.roll(x, ROWS - 1, 1))
        sides = pltpu.roll(x, 1, 2) + pltpu.roll(x, nz - 1, 2)
        beside = (up + down) + sides + (inside + take(far, slots[4]))
        out[pl.ds(j * ROWS, g * ROWS), :] = (6.0 * x - beside).reshape(g * ROWS, nz)
    if edge:
        for i, (ref, slot, y) in enumerate(((nxt, slots[2], ROWS - 1), (prev, slots[0], 0))):
            got = ref[pl.ds(slot * n * ROWS + y, n, stride=ROWS), :]
            out[pl.ds(n * ROWS + i * ceil_to(n, 8), n), :] = got


def couple(n, chunk, blocks, fields, matrix, lap, rhs, mixed, emit):
    nz = lap.shape[1]
    kl = fields.shape[0]
    wide, tall = ceil_to(n, 16), ceil_to(n, 8)
    used = pl.ds(0, blocks * kl * tall)
    for part in range(ROWS // TOGETHER):
        slot = part % SLOTS
        for half in range(TOGETHER):
            v = lap[pl.ds(TOGETHER * part + half, n, stride=ROWS), :]
            hi = v.astype(BF16)
            lo = (v - hi.astype(F32)).astype(BF16)
            cols = pl.ds(half * nz, nz)
            rhs[slot, pl.ds(0, n), cols] = hi
            rhs[slot, pl.ds(wide, n), cols] = lo
            rhs[slot, pl.ds(2 * wide, n), cols] = hi
        mixed[slot] = jnp.dot(matrix[used, :], rhs[slot], preferred_element_type=F32)
        for half in range(TOGETHER):
            y = TOGETHER * part + half
            cols = pl.ds(half * nz, nz)
            for b in range(blocks):
                total = None
                for k in range(kl):
                    field = fields[k, pl.ds(chunk * ROWS + y, 1), :]
                    at = pl.ds((b * kl + k) * tall, n)
                    term = field * mixed[slot, at, cols]
                    total = term if total is None else total + term
                emit(y, b, total)


def clear_rhs(n, rhs):
    if ceil_to(n, 16) != n:
        rhs[...] = jnp.zeros_like(rhs)


def own_kernel(n, chunk, blocks, fields, matrices, lap, out, rhs, mixed):
    clear_rhs(n, rhs)

    def emit(y, b, total):
        out[pl.ds(b * n * ROWS + y, n, stride=ROWS), :] = total

    couple(n, chunk, blocks, fields, matrices.at[0], lap, rhs, mixed, emit)


def final_kernel(n, entries, last, double, *refs):
    fields, slope, average, metal, matrices, source = refs[:6]
    refs = refs[6:]
    groups = []
    for chunk, slot, has_own, others in entries:
        size = 2 + has_own + others
        groups.append((chunk, slot, has_own, refs[:size]))
        refs = refs[size:]
    blended, refs = (refs[0], refs[1:]) if double else (None, refs)
    outs, (rhs, mixed, sums) = refs[:-3], refs[-3:]
    outs = outs[2:] if len(outs) == 4 else outs
    clear_rhs(n, rhs)
    g = group_of(n)
    for index, (chunk, slot, has_own, (field, lap, *laps)) in enumerate(groups):
        nz = lap.shape[1]
        base = laps[0] if has_own else None
        laps = laps[1:] if has_own else [lap, *laps]
        for other, received in enumerate(laps):

            def emit(y, b, total):
                at = pl.ds(b * n * ROWS + y, n, stride=ROWS)
                sums[at, :] = total if base is None else base[at, :] + total

            couple(
                n,
                chunk,
                2 if double else 1,
                fields,
                matrices.at[other + has_own],
                received,
                rhs,
                mixed,
                emit,
            )
            base = sums
        here, cond, step = cell_factors(chunk, slope, average, metal)
        rows_here = pl.ds(index * ROWS, ROWS)
        for j in range(0, n, g):

            def take(ref, part=0):
                rows = pl.ds((part * n + j) * ROWS, g * ROWS)
                return ref[rows, :].reshape(g, ROWS, nz)

            u = take(field, slot)
            rest = here * u + (cond * take(lap) + take(sums))
            residual = source[pl.ds(j, g), rows_here, :] - rest
            u = u + step * residual
            if last:
                outs[0][pl.ds(j, g), rows_here, :] = u
                outs[1][pl.ds(j, g), rows_here, :] = residual
            else:
                outs[0][pl.ds(j * ROWS, g * ROWS), :] = u.reshape(g * ROWS, nz)
            if double:
                u = take(blended) - step * (cond * take(laps[0]) + take(sums, 1))
                outs[0][pl.ds((n + j) * ROWS, g * ROWS), :] = u.reshape(g * ROWS, nz)


def matrices_kernel(n, count, blocks, me, pairs, entries, out):
    kl, _, listed = pairs.shape
    wide, tall = ceil_to(n, 16), ceil_to(n, 8)
    row = lax.broadcasted_iota(jnp.int32, (tall, listed), 0)
    column = lax.broadcasted_iota(jnp.int32, (wide, listed), 0)
    starts = [lax.rem(me[0] - s + count, count) * n for s in range(count)]
    columns = jnp.concatenate(
        [jnp.where(column < n, start + column, -1) for start in starts], axis=0
    )
    for k in range(kl):
        hits = jnp.where(columns == pairs[k, pl.ds(1, 1), :], 1.0, 0.0).astype(BF16)
        for b in range(blocks):
            rows = jnp.where(row < n, starts[b] + row, -1)
            value = jnp.broadcast_to(entries[pl.ds(k, 1), :], (tall, listed))
            value = jnp.where(rows == pairs[k, pl.ds(0, 1), :], value, 0.0)
            parts = []
            for _ in range(3):
                part = value.astype(BF16)
                value = value - part.astype(F32)
                parts.append(part)
            sums = lax.dot_general(
                jnp.concatenate(parts, axis=0),
                hits,
                (((1,), (1,)), ((), ())),
                preferred_element_type=F32,
            )
            g = sums[:tall] + sums[tall : 2 * tall] + sums[2 * tall :]
            hi = g.astype(BF16)
            lo = (g - hi.astype(F32)).astype(BF16)
            for s in range(count):
                at = slice(s * wide, (s + 1) * wide)
                out[s, pl.ds((b * kl + k) * tall, tall), :] = jnp.concatenate(
                    [hi[:, at], hi[:, at], lo[:, at]], axis=1
                )


def whole(a):
    return pl.BlockSpec(a.shape, lambda i, d=len(a.shape): (0,) * d)


def estimate(flops, moved):
    return pl.CostEstimate(flops=flops, bytes_accessed=4 * moved, transcendentals=0)


def scratch(n, blocks, kl, nz):
    wide, tall = ceil_to(n, 16), ceil_to(n, 8)
    return [
        pltpu.VMEM((SLOTS, 3 * wide, TOGETHER * nz), BF16),
        pltpu.VMEM((SLOTS, blocks * kl * tall, TOGETHER * nz), F32),
    ]


def lap_call(n, chunk, prev, cur, nxt, near, far, edge=False, compact=False):
    arrays, slots = zip(prev, cur, nxt, near, far)
    nz = cur[0].shape[1]
    rows = n * ROWS + (2 * ceil_to(n, 8) if edge else 0)
    return pl.pallas_call(
        functools.partial(lap_kernel, n, chunk, slots, edge, compact),
        out_shape=jax.ShapeDtypeStruct((rows, nz), F32),
        in_specs=[vmem()] * 5,
        out_specs=vmem(),
        compiler_params=params(),
        name="lap",
        cost_estimate=estimate(12 * rows * nz, 6 * rows * nz),
    )(*arrays)


def own_call(n, chunk, blocks, fields, matrices, lap):
    kl, _, nz = fields.shape
    size = n * ROWS * nz
    return pl.pallas_call(
        functools.partial(own_kernel, n, chunk, blocks),
        out_shape=jax.ShapeDtypeStruct((blocks * n * ROWS, nz), F32),
        in_specs=[vmem()] * 3,
        out_specs=vmem(),
        scratch_shapes=scratch(n, blocks, kl, nz),
        compiler_params=params(),
        name="own",
        cost_estimate=estimate(6 * blocks * kl * n * size, 2 * size),
    )(fields, matrices, lap)


def final_call(n, chunks, last, shared, matrices, source, parts, blended, outs):
    nz = source.shape[2]
    double = blended is not None
    blocks = 2 if double else 1
    block = pl.BlockSpec(
        (n, len(chunks) * ROWS, nz), lambda i: (0, chunks[0] // len(chunks), 0)
    )
    operands, entries = [*shared, matrices, source], []
    for chunk, (field, lap, own, laps) in zip(chunks, parts):
        entries.append((chunk, field[1], own is not None, len(laps)))
        operands += [field[0], lap, *([] if own is None else [own]), *laps]
    operands += [blended] if double else []
    specs = [block if a is source else whole(a) for a in operands]
    aliases = {}
    if last:
        shapes = [jax.ShapeDtypeStruct(source.shape, F32)] * 2
        out_specs = [block] * 2
        if outs:
            aliases = {len(operands) + i: i for i in range(2)}
            operands += list(outs)
            specs += [pl.BlockSpec(memory_space=pl.ANY)] * 2
    else:
        shapes = [jax.ShapeDtypeStruct((blocks * n * ROWS, nz), F32)]
        out_specs = [whole(shapes[0])]
    size = len(chunks) * n * ROWS * nz
    kl = shared[0].shape[0]
    return pl.pallas_call(
        functools.partial(final_kernel, n, tuple(entries), last, double),
        grid=(1,),
        out_shape=shapes,
        in_specs=specs,
        out_specs=out_specs,
        scratch_shapes=[
            *scratch(n, blocks, kl, nz),
            pltpu.VMEM((blocks * n * ROWS, nz), F32),
        ],
        input_output_aliases=aliases,
        compiler_params=params(),
        name="final",
        cost_estimate=estimate(6 * blocks * kl * n * size, 6 * size),
    )(*operands)


def coupling(pairs, entries, n, blocks):
    count = lax.axis_size("modes")
    me = lax.axis_index("modes").astype(jnp.int32).reshape(1)
    kl, listed = entries.shape
    wide, tall = ceil_to(n, 16), ceil_to(n, 8)
    shape = (count, blocks * kl * tall, 3 * wide)
    return pl.pallas_call(
        functools.partial(matrices_kernel, n, count, blocks),
        out_shape=jax.ShapeDtypeStruct(shape, BF16),
        in_specs=[pl.BlockSpec(memory_space=pltpu.SMEM), vmem(), vmem()],
        out_specs=vmem(),
        compiler_params=params(),
        name="coupling",
        cost_estimate=estimate(2 * listed * shape[0] * shape[1] * shape[2], 10000),
    )(me, pairs.transpose(0, 2, 1), entries)


def near_swap(x):
    count = lax.axis_size("space")
    return lax.ppermute(x, "space", [(i, i ^ 1) for i in range(count)])


def far_swap(x):
    count = lax.axis_size("space")
    pairs = [(i, (i + (1 if i % 2 else -1)) % count) for i in range(count)]
    return lax.ppermute(x, "space", pairs)


def to_others(x):
    count = lax.axis_size("modes")
    got = []
    for s in range(1, count):
        ring = [(i, (i + s) % count) for i in range(count)]
        got.append(lax.ppermute(x, "modes", ring))
    return got


FINALS = ((1,), (0,), (2, 3))


def doubled(count, devices):
    return count == 4 and devices == 2


def rounds(n, count, u0, source, shared, pairs, entries):
    nz = u0.shape[-1]
    double = doubled(count, lax.axis_size("modes"))
    tail = count - 1
    cut = lambda c: u0[:, c * ROWS : (c + 1) * ROWS].reshape(n * ROWS, nz)
    field = {0: (cut(0), 0)}
    u0, first = lax.optimization_barrier((u0, field[0][0]))
    field[0] = (first, 0)
    for c in range(1, count):
        field[c] = (cut(c), 0)
    matrices = coupling(pairs, entries, n, 2 if double else 1)
    near_whole = near_swap(u0)
    blended = None
    if double:
        _, slope, average, metal = (a[..., tail * ROWS : count * ROWS, :] for a in shared)
        step = RELAXATION / (slope + 6.0 * average * (1.0 + 3.0 * metal.astype(F32)))
        u = u0[:, tail * ROWS : count * ROWS]
        v = u + step * (source[:, tail * ROWS : count * ROWS] - slope * u)
        blended = v.reshape(n * ROWS, nz)
        (blended,) = to_others(blended)
    outs = ()
    for turn in range(ROUNDS):
        last = turn == ROUNDS - 1
        near, far, parts = {}, {}, {}
        for c in range(count):
            if turn:
                near[c] = (near_swap(field[c][0]), 0)
            else:
                near[c] = (near_whole, 0)
            far[c] = (far_swap(field[c][0]), 0)
        for c in range(count):
            both = double and c == tail
            prev, nxt = field[(c - 1) % count], field[(c + 1) % count]
            edge = double and last and c == tail - 2
            lap = lap_call(n, c, prev, field[c], nxt, near[c], far[c], edge)
            if both and last:
                of_other = lambda a: (a[0], 1)
                handed = (parts[tail - 2][3][0], 0)
                laps = [
                    lap_call(
                        n,
                        c,
                        handed,
                        of_other(field[c]),
                        handed,
                        of_other(near[c]),
                        of_other(far[c]),
                        compact=True,
                    )
                ]
            else:
                laps = to_others(lap)
            own = None
            if not (both and last):
                blocks = 2 if both else 1
                own = own_call(n, c, blocks, shared[0], matrices, lap)
            parts[c] = (field[c], lap, own, laps)
        new = {}
        for chunks in FINALS if last and double else [(c,) for c in range(count)]:
            c = chunks[0]
            given = blended if double and c == tail and not last else None
            got = final_call(
                n,
                chunks,
                last,
                shared,
                matrices,
                source,
                [parts[d] for d in chunks],
                given,
                outs,
            )
            if last:
                outs = got
            else:
                new[c] = (got[0], 0)
        field = new
    return outs


def on_device(
    initial_heat_weights,
    source_weights,
    heat_storage_slope,
    average_diffusivity,
    metal_indicator,
    uncertain_diffusivity_fields,
    basis_index_pairs,
    basis_integral_entries,
):
    n, planes, ny, _ = initial_heat_weights.shape
    assert planes == 1 and ny % ROWS == 0
    u0 = initial_heat_weights[:, 0]
    source = source_weights[:, 0]
    shared = (
        uncertain_diffusivity_fields[:, 0],
        heat_storage_slope[0],
        average_diffusivity[0],
        metal_indicator[0],
    )
    outs = rounds(
        n, ny // ROWS, u0, source, shared, basis_index_pairs, basis_integral_entries
    )
    return (outs[0][:, None], outs[1][:, None])


def solution(mesh):
    placed = (
        P("modes", "space", None, None),
        P("modes", "space", None, None),
        P("space", None, None),
        P("space", None, None),
        P("space", None, None),
        P(None, "space", None, None),
        P(),
        P(),
    )
    return jax.shard_map(
        on_device,
        mesh=mesh,
        in_specs=placed,
        out_specs=(P("modes", "space", None, None), P("modes", "space", None, None)),
        check_vma=False,
    )
```
